32 devices in a mesh: rep: 2 (over y), req: 4 (over z), mp: 4 (over x, core).
Axes of the slice: x: 2, y: 2, z: 4, core: 2. Of those that a mesh axis runs over, the one named last changes fastest.
Arguments:
- hidden_in: bfloat16 [128, 2, 8192], P(('rep', 'req'), None, 'mp'), parts along dimension 0, may hold values from -6 to 6
- frozen_query_rows: bfloat16 [128, 2, 8192], P(('rep', 'req'), None, 'mp'), parts along dimension 0, may hold values from -6 to 86
- new_kv: bfloat16 [128, 2, 2, 1024], P(('rep', 'req'), None, None, 'mp'), parts along dimension 0, may hold values from -6 to 31
- adapter_of: int32 [128], P(('rep', 'req')), parts along dimension 0, may hold values from 0 to 7, as said below
- adapter_home: int32 [16], P('rep'), parts along dimension 0, may hold values from 0 to 7, as said below
- a_store: bfloat16 [16, 64, 8192], P(('rep', 'req'), None, 'mp'), parts along dimension 0, may hold values from -0.0625 to 0.0625
- b_store: bfloat16 [16, 64, 8192], P(('rep', 'req'), None, 'mp'), parts along dimension 0, may hold values from -0.75 to 0.75
- kv_pool: bfloat16 [2, 1024, 16, 1024], P(None, ('rep', 'req'), None, 'mp'), parts along dimension 1, may hold values from -6 to 31
- page_table: int32 [128, 8], P(('rep', 'req')), parts along dimension 0, may hold values from 0 to 127, as said below
- cached_len: int32 [128], P(('rep', 'req')), parts along dimension 0, may hold values from 32 to 128
- new_group: int32 [128], P(('rep', 'req')), parts along dimension 0, may hold values from 0 to 3, as said below
Outputs:
- attended: bfloat16 [128, 2, 8192], P(('rep', 'req'), None, 'mp'), parts along dimension 0
- cache: bfloat16 [2, 128, 128, 1024], P(None, ('rep', 'req'), None, 'mp'), parts along dimension 1
The draws below stay inside these ranges and needn't reach their ends.
There are 2 independent parts, one for each index of `rep`. The reference program is written for one: setup_inputs(seed, part) draws one part's arguments, and reference() takes and returns one part's arrays. A program takes and returns all parts, laid end to end along the dimension named above; each array names one. Nothing has to cross between parts.
Inputs may be any that keep to these rules, and one draw needn't show every extreme that they name: A permutation: adapter a lives in store slot adapter_home[a], which belongs to group adapter_home[a] div 2. `adapter_of`: the requests of one group (new rows h * 16 to h * 16 + 15) use adapters of min(16, number of groups) different owners, at most 4 requests an owner, a number reached in every group; all requests of one group whose adapters have one owner use the same adapter. `page_table`: the rows of one group name each of its 128 pages once. `new_group`: A request keeps its slot (row mod 16); the same 4 slots keep their group in every group; every group receives exactly one request into each slot; no group sends more than 3 requests to one other group, and some pair of groups reaches it.
All inputs are finite; a program needn't handle non-finite values.
Results may differ from the reference program's by a relative error of at most 0.0069.
Values may be sent and summed in bfloat16 or wider, within the bound.
A program may use at most 64 MiB of HBM per device.

```python
import jax
import jax.numpy as jnp
from jax import lax

D = 8192
HEAD = 128
RANK = 64
STEPS = 2
PAGE = 16
REQ_DEV = 16
CTX = 128
ADAPT_DEV = 2
QW = 8192
KVW = 1024
REQUESTS = 64
ADAPTERS = 8
PAGES_REQ = 8
POOL_DEV = 128
POOL = 512


def shared_home(key):
    return jax.random.permutation(jax.random.fold_in(key, 17), ADAPTERS).astype(jnp.int32)


def draw_adapter_home(key, part):
    return shared_home(key)


def draw_adapter_of(key, part):
    owner_count = ADAPTERS // ADAPT_DEV
    group_count = REQUESTS // REQ_DEV
    home_slots = shared_home(key)
    inverse = jnp.argsort(home_slots, stable=True).astype(jnp.int32)
    order_keys = jax.random.split(jax.random.fold_in(key, 23), group_count)
    owner_order = jax.vmap(lambda subkey: jax.random.permutation(subkey, owner_count))(order_keys)
    slot_keys = jax.random.split(jax.random.fold_in(key, 29), group_count)
    slot_order = jax.vmap(lambda subkey: jax.random.permutation(subkey, REQ_DEV))(slot_keys)
    owners = jnp.take_along_axis(owner_order, slot_order % owner_count, axis=1)
    local_pick = jax.random.randint(jax.random.fold_in(key, 31), (group_count, owner_count), 0, ADAPT_DEV)
    chosen = jnp.take_along_axis(local_pick, owners, axis=1)
    return inverse[(owners * ADAPT_DEV + chosen).reshape(-1)].astype(jnp.int32)


def draw_new_group(key, part):
    group_count = REQUESTS // REQ_DEV
    stay_count = REQ_DEV // 4
    spread = jax.random.permutation(jax.random.fold_in(key, 37), group_count)
    target = jax.random.permutation(jax.random.fold_in(key, 41), group_count)
    slot_rank = jax.random.permutation(jax.random.fold_in(key, 43), REQ_DEV)
    group_ids = jnp.arange(group_count)[:, None]
    moved = target[(spread[group_ids] + slot_rank[None, :]) % group_count]
    return jnp.where(slot_rank[None, :] < stay_count, group_ids, moved).reshape(-1).astype(jnp.int32)


def draw_page_table(key, part):
    group_count = REQUESTS // REQ_DEV
    page_keys = jax.random.split(jax.random.fold_in(key, 47), group_count)
    perms = jax.vmap(lambda subkey: jax.random.permutation(subkey, POOL_DEV))(page_keys)
    return perms.reshape(REQUESTS, PAGES_REQ).astype(jnp.int32)


def draw_cached_len(key, part):
    lengths = jax.random.randint(jax.random.fold_in(key, 53), (REQUESTS,), CTX // 4, CTX + 1)
    return lengths.at[0].set(CTX).at[1].set(CTX // 4).astype(jnp.int32)


def draw_frozen_query_rows(key, part):
    q_shape = (REQUESTS, STEPS, QW)
    return jnp.clip(jax.random.normal(jax.random.fold_in(key, 1), q_shape), -6.0, 6.0).astype(jnp.bfloat16)


def draw_kv_pool(key, part):
    pool_shape = (2, POOL, PAGE, KVW)
    return jnp.clip(jax.random.normal(jax.random.fold_in(key, 4), pool_shape), -6.0, 6.0).astype(jnp.bfloat16)


def draw_new_kv(key, part):
    kv_shape = (REQUESTS, STEPS, 2, KVW)
    return jnp.clip(jax.random.normal(jax.random.fold_in(key, 8), kv_shape), -6.0, 6.0).astype(jnp.bfloat16)


def level_of(key, extent, cuts, least, high):
    loudness = 1.0
    for position, blocks in cuts:
        steps = jax.random.uniform(jax.random.fold_in(jax.random.fold_in(key, 6), position), (blocks,), jnp.float32, least / len(cuts), high / len(cuts))
        loudness = loudness * jnp.repeat(jnp.exp(steps), extent[position] // blocks).reshape((-1,) + (1,) * (len(extent) - 1 - position))
    return loudness


def normal_values(key, shape, scale, bound, shards=(), held_as=jnp.bfloat16):
    factor_of = level_of(key, shape, shards, -0.22, 0.18) if shards else 1.0
    result = jax.random.normal(key, shape, jnp.float32) * scale * factor_of
    return jnp.minimum(jnp.maximum(result, -bound), bound).astype(held_as)


def setup_inputs(seed: int = 0, part: int = 0) -> dict:
    arg_keys = jax.random.split(jax.random.key(seed), 12)
    part_splits = jax.random.split(jax.random.fold_in(arg_keys[11], part), 12)
    return {
        "hidden_in": normal_values(part_splits[0], (REQUESTS, STEPS, D), 1.0, 6.0, ((0, 4), (2, 4))),
        "frozen_query_rows": draw_frozen_query_rows(jax.random.fold_in(jax.random.fold_in(arg_keys[11], part), 71), part),
        "new_kv": draw_new_kv(jax.random.fold_in(jax.random.fold_in(arg_keys[11], part), 71), part),
        "adapter_of": draw_adapter_of(jax.random.fold_in(jax.random.fold_in(arg_keys[11], part), 71), part),
        "adapter_home": draw_adapter_home(jax.random.fold_in(jax.random.fold_in(arg_keys[11], part), 71), part),
        "a_store": normal_values(part_splits[5], (ADAPTERS, RANK, D), D ** -0.5, 0.0625, ((0, 4), (2, 4))),
        "b_store": normal_values(part_splits[6], (ADAPTERS, RANK, QW), RANK ** -0.5, 0.75, ((0, 4), (2, 4))),
        "kv_pool": draw_kv_pool(jax.random.fold_in(jax.random.fold_in(arg_keys[11], part), 71), part),
        "page_table": draw_page_table(jax.random.fold_in(jax.random.fold_in(arg_keys[11], part), 71), part),
        "cached_len": draw_cached_len(jax.random.fold_in(jax.random.fold_in(arg_keys[11], part), 71), part),
        "new_group": draw_new_group(jax.random.fold_in(jax.random.fold_in(arg_keys[11], part), 71), part),
    }


NEG_FILL = -1.0e30


def attend(query_vectors, cached_keys, cached_values, length, fresh_kv):
    row_count, step_count, q_width = query_vectors.shape
    context = cached_keys.shape[1]
    kv_width = cached_keys.shape[2]
    kv_heads = kv_width // HEAD
    per_kv = q_width // kv_width
    score_scale = HEAD ** -0.5
    q_split = query_vectors.reshape(row_count, step_count, kv_heads, per_kv, HEAD)
    k_split = cached_keys.reshape(row_count, context, kv_heads, HEAD)
    v_split = cached_values.reshape(row_count, context, kv_heads, HEAD)
    new_keys = fresh_kv[:, :, 0].reshape(row_count, step_count, kv_heads, HEAD)
    new_values = fresh_kv[:, :, 1].reshape(row_count, step_count, kv_heads, HEAD)
    old_scores = jnp.einsum("bskgd,bjkd->bskgj", q_split, k_split, preferred_element_type=jnp.float32) * score_scale
    visible = jnp.arange(context)[None, :] < length[:, None]
    old_scores = jnp.where(visible[:, None, None, None, :], old_scores, NEG_FILL)
    new_scores = jnp.einsum("bskgd,btkd->bskgt", q_split, new_keys, preferred_element_type=jnp.float32) * score_scale
    causal = jnp.arange(step_count)[None, :] <= jnp.arange(step_count)[:, None]
    new_scores = jnp.where(causal[None, :, None, None, :], new_scores, NEG_FILL)
    scores = jnp.concatenate([old_scores, new_scores], axis=-1)
    row_max = jnp.max(scores, axis=-1, keepdims=True)
    weights = jnp.exp(scores - row_max)
    probabilities = (weights / jnp.sum(weights, axis=-1, keepdims=True)).astype(jnp.bfloat16)
    attention_out = jnp.einsum("bskgj,bjkd->bskgd", probabilities[..., :context], v_split, preferred_element_type=jnp.float32)
    attention_out = attention_out + jnp.einsum("bskgt,btkd->bskgd", probabilities[..., context:], new_values, preferred_element_type=jnp.float32)
    return attention_out.reshape(row_count, step_count, q_width).astype(jnp.bfloat16)


def reference(hidden_in, frozen_query_rows, new_kv, adapter_of, adapter_home, a_store, b_store, kv_pool, page_table, cached_len, new_group):
    old_rows = jnp.arange(REQUESTS, dtype=jnp.int32)
    new_rows = (new_group * REQ_DEV + old_rows % REQ_DEV).astype(jnp.int32)
    source = jnp.zeros((REQUESTS,), jnp.int32).at[new_rows].set(old_rows)

    def per_request(fresh_position_row):
        old_row = source[fresh_position_row]
        store_slot = adapter_home[adapter_of[fresh_position_row]]
        panel_a = a_store[store_slot]
        up_projection_panel = b_store[store_slot]
        complete_rank_product = jnp.dot(hidden_in[fresh_position_row], panel_a.T, preferred_element_type=jnp.float32).astype(jnp.bfloat16)
        adapter_query_delta = jnp.dot(complete_rank_product, up_projection_panel, preferred_element_type=jnp.float32)
        query_vectors = (frozen_query_rows[fresh_position_row].astype(jnp.float32) + adapter_query_delta).astype(jnp.bfloat16)
        page_ids = ((old_row // REQ_DEV) * POOL_DEV + page_table[old_row]).astype(jnp.int32)
        kv_pages = jnp.take(kv_pool, page_ids, axis=1).reshape(2, CTX, KVW)
        attended_row = attend(query_vectors[None], kv_pages[0][None], kv_pages[1][None], cached_len[old_row][None], new_kv[fresh_position_row][None])[0]
        return attended_row, kv_pages

    attended, cache_rows = lax.map(per_request, old_rows)
    cache = jnp.transpose(cache_rows, (1, 0, 2, 3))
    return (attended, cache)
```

```python
import functools

import jax
import jax.numpy as jnp
from jax import lax
from jax.experimental import pallas as pl
from jax.experimental.pallas import tpu as pltpu
from jax.sharding import PartitionSpec as P

HEAD = 128
NEG_FILL = -1e30
MESH = pl.DeviceIdType.MESH
VMEM = pltpu.VMEM
SMEM = pltpu.SMEM


def kernel(
    cfg,
    adapter_of,
    adapter_home,
    page_table,
    cached_len,
    new_group,
    hidden,
    frozen,
    fresh,
    a_panels,
    b_panels,
    pool,
    att_out,
    cache_out,
    h_send,
    h_all,
    f_send,
    f_all,
    r_part,
    r_all,
    q_send,
    q_all,
    q_rows,
    meta_send,
    meta_all,
    meta_s,
    page_send,
    rows,
    att,
    h_ss,
    h_rs,
    f_ss,
    f_rs,
    r_ss,
    r_rs,
    q_ss,
    q_rs,
    m_ss,
    m_rs,
    p_ss,
    p_rs,
    l_sem,
):
    groups, mps, per_group, steps, cap, block, store_count, rank, pages, page, move_cap = cfg
    f32, bf16 = jnp.float32, jnp.bfloat16
    rep = lax.axis_index("rep")
    me = lax.axis_index("req")
    mp = lax.axis_index("mp")
    width = hidden.shape[1]
    lanes = store_count * rank
    kv_width = pool.shape[3]
    kv_heads = kv_width // HEAD
    per_kv = width // kv_width
    context = pages * page
    sent_rows = groups * block
    own_rows = per_group * steps

    def peer(d):
        return lax.rem(me + d, groups)

    def send_to(d):
        return (rep, peer(d), mp)

    barrier = pltpu.get_barrier_semaphore()
    for d in range(1, groups):
        pl.semaphore_signal(barrier, inc=1, device_id=send_to(d), device_id_type=MESH)
    for d in range(1, mps):
        pl.semaphore_signal(
            barrier, inc=1, device_id=(rep, me, lax.rem(mp + d, mps)), device_id_type=MESH
        )

    owners, picks, targets = [], [], []
    for r in range(per_group):
        home = adapter_home[adapter_of[r]]
        owner = home // store_count
        picks.append(home - owner * store_count)
        place = jnp.int32(0)
        for o in owners:
            place = place + (o == owner).astype(jnp.int32)
        owners.append(owner)
        targets.append(owner * block + place * steps)
    col = lax.broadcasted_iota(jnp.int32, (sent_rows, own_rows), 1)
    row = lax.broadcasted_iota(jnp.int32, (sent_rows, own_rows), 0)
    want = jnp.zeros((sent_rows, own_rows), jnp.int32)
    mrow = lax.broadcasted_iota(jnp.int32, (own_rows, lanes), 0) // steps
    mlane = lax.broadcasted_iota(jnp.int32, (own_rows, lanes), 1) // rank
    mpick = jnp.zeros((own_rows, lanes), jnp.int32)
    for r in range(per_group):
        want = jnp.where(col // steps == r, targets[r] + lax.rem(col, steps), want)
        mpick = jnp.where(mrow == r, picks[r], mpick)
    pick_by_owner = (row == want).astype(f32).astype(bf16)
    mask = (mlane == mpick).astype(f32).astype(bf16)

    h_out = jnp.dot(pick_by_owner, hidden[...], preferred_element_type=f32)
    m_out = jnp.dot(pick_by_owner, mask, preferred_element_type=f32)
    h_send[:, :, :width] = h_out.reshape(groups, block, width).astype(bf16)
    h_send[:, :, width:] = m_out.reshape(groups, block, lanes).astype(bf16)
    mi = lax.broadcasted_iota(jnp.int32, (8, 128), 0)
    mj = lax.broadcasted_iota(jnp.int32, (8, 128), 1)
    meta = jnp.zeros((8, 128), jnp.int32)
    for r in range(per_group):
        meta = jnp.where((mi == 0) & (mj == r), new_group[r], meta)
        meta = jnp.where((mi == 1) & (mj == r), cached_len[r], meta)
    meta_send[...] = meta

    pl.semaphore_wait(barrier, groups - 1 + mps - 1)

    def copies(src, dst, ss, rs):
        out = {}
        for d in range(1, groups):
            out[d] = pltpu.make_async_remote_copy(
                src_ref=src(d),
                dst_ref=dst,
                send_sem=ss.at[d - 1],
                recv_sem=rs.at[d - 1],
                device_id=send_to(d),
                device_id_type=MESH,
            )
        return out

    h_cp = copies(lambda d: h_send.at[peer(d)], h_all.at[me], h_ss, h_rs)
    order = sorted(range(1, groups), key=lambda d: -min(d, groups - d))
    for d in order:
        h_cp[d].start()
    h_all[me] = h_send[me]

    f_out = jnp.dot(pick_by_owner, frozen[...], preferred_element_type=f32)
    f_send[...] = f_out.reshape(groups, block, width).astype(bf16)
    f_cp = copies(lambda d: f_send.at[peer(d)], f_all.at[me], f_ss, f_rs)
    for d in order:
        f_cp[d].start()
    f_all[me] = f_send[me]
    m_cp = copies(lambda d: meta_send, meta_all.at[me], m_ss, m_rs)
    for d in order:
        m_cp[d].start()
    meta_all[me] = meta

    p_cp = {}
    for d in order:
        dest = peer(d)
        count = jnp.int32(0)
        sources = [jnp.int32(0)] * move_cap
        for r in range(per_group):
            hit = new_group[r] == dest
            for k in range(move_cap):
                sources[k] = jnp.where(hit & (count == k), r, sources[k])
            count = count + hit.astype(jnp.int32)
        for k in range(move_cap):
            slot = (d - 1) * move_cap + k
            for j in range(pages):
                page_id = page_table[sources[k] * pages + j]
                page_send[slot, :, pl.ds(j * page, page), :] = pool[:, page_id]
            p_cp[slot] = pltpu.make_async_remote_copy(
                src_ref=page_send.at[slot],
                dst_ref=rows.at[per_group + slot],
                send_sem=p_ss.at[slot],
                recv_sem=p_rs.at[slot],
                device_id=send_to(d),
                device_id_type=MESH,
            )
            p_cp[slot].start()

    for d in range(1, groups):
        h_cp[d].wait_recv()
    h_in = h_all[...].astype(f32).reshape(sent_rows, width + lanes)
    part = lax.dot_general(
        h_in[:, :width].astype(bf16),
        a_panels[...],
        (((1,), (1,)), ((), ())),
        preferred_element_type=f32,
    )
    r_part[...] = part * h_in[:, width:]
    r_cp = {}
    for d in range(1, mps):
        r_cp[d] = pltpu.make_async_remote_copy(
            src_ref=r_part,
            dst_ref=r_all.at[mp],
            send_sem=r_ss.at[d - 1],
            recv_sem=r_rs.at[d - 1],
            device_id=(rep, me, lax.rem(mp + d, mps)),
            device_id_type=MESH,
        )
        r_cp[d].start()
    r_all[mp] = r_part[...]

    @pl.loop(0, per_group)
    def _(r):
        for j in range(pages):
            rows[r, :, pl.ds(j * page, page), :] = pool[:, page_table[r * pages + j]]

    for d in range(1, mps):
        r_cp[d].wait_recv()
    total = r_all[0]
    for j in range(1, mps):
        total = total + r_all[j]
    for d in range(1, groups):
        f_cp[d].wait_recv()
    delta = jnp.dot(total.astype(bf16), b_panels[...], preferred_element_type=f32)
    q_done = f_all[...].astype(f32) + delta.reshape(groups, block, width)
    q_send[...] = q_done.astype(bf16)
    q_cp = copies(lambda d: q_send.at[peer(d)], q_all.at[me], q_ss, q_rs)
    for d in order:
        q_cp[d].start()
    q_all[me] = q_send[me]

    for d in range(1, groups):
        m_cp[d].wait_recv()
    local = pltpu.make_async_copy(meta_all, meta_s, l_sem)
    local.start()
    local.wait()
    entry_slot = [jnp.int32(r) for r in range(per_group)]
    entry_len = [cached_len[r] for r in range(per_group)]
    source = [jnp.int32(r) for r in range(per_group)]
    for d in range(1, groups):
        origin = lax.rem(me + groups - d, groups)
        count = jnp.int32(0)
        slots = [jnp.int32(0)] * move_cap
        for r in range(per_group):
            hit = meta_s[origin, 0, r] == me
            for k in range(move_cap):
                slots[k] = jnp.where(hit & (count == k), r, slots[k])
            source[r] = jnp.where(
                hit,
                per_group + (d - 1) * move_cap + jnp.minimum(count, move_cap - 1),
                source[r],
            )
            count = count + hit.astype(jnp.int32)
        for k in range(move_cap):
            entry_slot.append(slots[k])
            entry_len.append(meta_s[origin, 1, slots[k]])

    for d in range(1, groups):
        q_cp[d].wait_recv()
    q_in = q_all[...].astype(f32).reshape(sent_rows, width)
    qr = per_kv * steps
    ri = lax.broadcasted_iota(jnp.int32, (qr, per_kv * sent_rows), 0)
    ci = lax.broadcasted_iota(jnp.int32, (qr, per_kv * sent_rows), 1)
    base = ci - (ri // steps) * sent_rows - lax.rem(ri, steps)
    place = jnp.concatenate(
        [(base == targets[r]).astype(f32) for r in range(per_group)], axis=0
    ).astype(bf16)
    for h in range(kv_heads):
        stack = jnp.concatenate(
            [
                q_in[:, (h * per_kv + i) * HEAD : (h * per_kv + i + 1) * HEAD]
                for i in range(per_kv)
            ],
            axis=0,
        ).astype(bf16)
        got = jnp.dot(place, stack, preferred_element_type=f32)
        q_rows[:, h] = got.reshape(per_group, qr, HEAD).astype(bf16)

    scale = HEAD ** (-0.5)
    step_of = lax.rem(lax.broadcasted_iota(jnp.int32, (qr, 1), 0), steps)
    position = lax.broadcasted_iota(jnp.int32, (qr, context), 1)

    def attend(entry, slot, length):
        new = fresh[slot].astype(f32)
        for h in range(kv_heads):
            cols = slice(h * HEAD, (h + 1) * HEAD)
            q = q_rows[slot, h]
            keys = rows[entry, 0, :, cols]
            values = rows[entry, 1, :, cols]
            s = (
                lax.dot_general(
                    q, keys, (((1,), (1,)), ((), ())), preferred_element_type=f32
                )
                * scale
            )
            s = jnp.where(position < length, s, NEG_FILL)
            top = jnp.max(s, axis=1, keepdims=True)
            qf = q.astype(f32)
            extra = []
            for t in range(steps):
                e = jnp.sum(qf * new[2 * t : 2 * t + 1, cols], axis=1, keepdims=True) * scale
                e = jnp.where(step_of >= t, e, NEG_FILL)
                extra.append(e)
                top = jnp.maximum(top, e)
            w = jnp.exp(s - top)
            norm = jnp.sum(w, axis=1, keepdims=True)
            extra = [jnp.exp(e - top) for e in extra]
            for e in extra:
                norm = norm + e
            prob = (w / norm).astype(bf16)
            o = jnp.dot(prob, values, preferred_element_type=f32)
            for t in range(steps):
                pe = (extra[t] / norm).astype(bf16).astype(f32)
                o = o + pe * new[2 * t + 1 : 2 * t + 2, cols]
            att[entry, h] = o.astype(bf16)

    for r in range(per_group):
        attend(r, r, entry_len[r])
    near = sorted(range(1, groups), key=lambda d: min(d, groups - d))
    for k in range(move_cap):
        for d in near:
            slot = (d - 1) * move_cap + k
            p_cp[slot].wait_recv()
            attend(
                per_group + slot, entry_slot[per_group + slot], entry_len[per_group + slot]
            )

    for r in range(per_group):
        cache_out[:, r] = rows[source[r]]
    pr = lax.broadcasted_iota(jnp.int32, (per_kv * own_rows, per_group * qr), 0)
    pc = lax.broadcasted_iota(jnp.int32, (per_kv * own_rows, per_group * qr), 1)
    in_row = lax.rem(pr, own_rows)
    spread = (
        pc == (in_row // steps) * qr + (pr // own_rows) * steps + lax.rem(in_row, steps)
    )
    spread = spread.astype(f32).astype(bf16)
    for h in range(kv_heads):
        stack = jnp.concatenate([att[source[r], h] for r in range(per_group)], axis=0)
        got = jnp.dot(spread, stack, preferred_element_type=f32).astype(bf16)
        for i in range(per_kv):
            att_out[:, (h * per_kv + i) * HEAD : (h * per_kv + i + 1) * HEAD] = got[
                i * own_rows : (i + 1) * own_rows
            ]

    for d in range(1, groups):
        h_cp[d].wait_send()
        f_cp[d].wait_send()
        m_cp[d].wait_send()
        q_cp[d].wait_send()
    for d in range(1, mps):
        r_cp[d].wait_send()
    for slot in p_cp:
        p_cp[slot].wait_send()


def per_device(
    hidden_in,
    frozen_query_rows,
    new_kv,
    adapter_of,
    adapter_home,
    a_store,
    b_store,
    kv_pool,
    page_table,
    cached_len,
    new_group,
):
    groups = lax.axis_size("req")
    mps = lax.axis_size("mp")
    per_group, steps, width = hidden_in.shape
    store_count, rank, _ = a_store.shape
    pages, page = page_table.shape[1], kv_pool.shape[2]
    kv_width = kv_pool.shape[3]
    context = pages * page
    move_cap = -(-(per_group - per_group // 4) // groups)
    cap = -(-per_group // min(16, groups))
    block = -(-cap * steps // 8) * 8
    lanes = store_count * rank
    qr = width // kv_width * steps
    kv_heads = kv_width // HEAD
    moved = (groups - 1) * move_cap
    entries = per_group + moved
    bf16, f32 = jnp.bfloat16, jnp.float32
    cfg = (groups, mps, per_group, steps, cap, block, store_count, rank, pages, page, move_cap)
    dma = pltpu.SemaphoreType.DMA
    att, cache = pl.pallas_call(
        functools.partial(kernel, cfg),
        out_shape=(
            jax.ShapeDtypeStruct((per_group * steps, width), bf16),
            jax.ShapeDtypeStruct((2, per_group, context, kv_width), bf16),
        ),
        in_specs=[pl.BlockSpec(memory_space=SMEM)] * 5 + [pl.BlockSpec(memory_space=VMEM)] * 6,
        out_specs=[pl.BlockSpec(memory_space=VMEM)] * 2,
        scratch_shapes=[
            VMEM((groups, block, width + lanes), bf16),
            VMEM((groups, block, width + lanes), bf16),
            VMEM((groups, block, width), bf16),
            VMEM((groups, block, width), bf16),
            VMEM((groups * block, lanes), f32),
            VMEM((mps, groups * block, lanes), f32),
            VMEM((groups, block, width), bf16),
            VMEM((groups, block, width), bf16),
            VMEM((per_group, kv_heads, qr, HEAD), bf16),
            VMEM((8, 128), jnp.int32),
            VMEM((groups, 8, 128), jnp.int32),
            SMEM((groups, 8, 128), jnp.int32),
            VMEM((moved, 2, context, kv_width), bf16),
            VMEM((entries, 2, context, kv_width), bf16),
            VMEM((entries, kv_heads, qr, HEAD), bf16),
            dma((groups - 1,)),
            dma((groups - 1,)),
            dma((groups - 1,)),
            dma((groups - 1,)),
            dma((mps - 1,)),
            dma((mps - 1,)),
            dma((groups - 1,)),
            dma((groups - 1,)),
            dma((groups - 1,)),
            dma((groups - 1,)),
            dma((moved,)),
            dma((moved,)),
            dma,
        ],
        compiler_params=pltpu.CompilerParams(
            collective_id=0, has_side_effects=True, vmem_limit_bytes=48 * 2**20
        ),
    )(
        adapter_of,
        adapter_home,
        page_table.reshape(-1),
        cached_len,
        new_group,
        hidden_in.reshape(per_group * steps, width),
        frozen_query_rows.reshape(per_group * steps, width),
        new_kv.reshape(per_group, steps * 2, kv_width),
        a_store.reshape(lanes, width),
        b_store.reshape(lanes, width),
        kv_pool,
    )
    return att.reshape(per_group, steps, width), cache


def solution(mesh):
    placed = (
        P(("rep", "req"), None, "mp"),
        P(("rep", "req"), None, "mp"),
        P(("rep", "req"), None, None, "mp"),
        P(("rep", "req")),
        P("rep"),
        P(("rep", "req"), None, "mp"),
        P(("rep", "req"), None, "mp"),
        P(None, ("rep", "req"), None, "mp"),
        P(("rep", "req"), None),
        P(("rep", "req")),
        P(("rep", "req")),
    )
    return jax.shard_map(
        per_device,
        mesh=mesh,
        in_specs=placed,
        out_specs=(P(("rep", "req"), None, "mp"), P(None, ("rep", "req"), None, "mp")),
        check_vma=False,
    )
```

```python
import functools

import jax
import jax.numpy as jnp
from jax import lax
from jax.experimental import pallas as pl
from jax.experimental.pallas import tpu as pltpu
from jax.sharding import PartitionSpec as P

HEAD = 128
NEG_FILL = -1e30
MESH = pl.DeviceIdType.MESH
VMEM = pltpu.VMEM
SMEM = pltpu.SMEM


def kernel(
    cfg,
    *refs,
):
    given, refs = refs[:11], refs[11:]
    body(cfg, given, refs[2:13], refs[13], *refs[:2], *refs[14:])


def body(
    cfg,
    given,
    held,
    in_sem,
    att_out,
    cache_out,
    h_send,
    h_all,
    f_send,
    f_all,
    r_part,
    r_all,
    q_send,
    q_all,
    q_rows,
    wide,
    meta_send,
    meta_all,
    meta_s,
    page_send,
    rows,
    att,
    h_ss,
    h_rs,
    f_ss,
    f_rs,
    r_ss,
    r_rs,
    q_ss,
    q_rs,
    m_ss,
    m_rs,
    p_ss,
    p_rs,
    l_sem,
):
    groups, mps, per_group, steps, cap, block, store_count, rank, pages, page, move_cap = cfg
    f32, bf16 = jnp.float32, jnp.bfloat16
    rep = lax.axis_index("rep")
    me = lax.axis_index("req")
    mp = lax.axis_index("mp")
    fetch = [
        pltpu.make_async_copy(src, dst, in_sem.at[i])
        for i, (src, dst) in enumerate(zip(given, held))
    ]
    for f in fetch:
        f.start()
    (
        adapter_of,
        adapter_home,
        page_table,
        cached_len,
        new_group,
        hidden,
        frozen,
        fresh,
        pool,
        a_panels,
        b_panels,
    ) = held
    width = hidden.shape[2]
    lanes = store_count * rank
    kv_width = pool.shape[3]
    kv_heads = kv_width // HEAD
    per_kv = width // kv_width
    context = pages * page
    sent_rows = groups * block
    own_rows = per_group * steps

    def peer(d):
        return lax.rem(me + d, groups)

    def send_to(d):
        return (rep, peer(d), mp)

    barrier = pltpu.get_barrier_semaphore()
    for d in range(1, groups):
        pl.semaphore_signal(barrier, inc=1, device_id=send_to(d), device_id_type=MESH)
    for d in range(1, mps):
        pl.semaphore_signal(
            barrier, inc=1, device_id=(rep, me, lax.rem(mp + d, mps)), device_id_type=MESH
        )

    for f in fetch[:6]:
        f.wait()

    owners, picks, targets = [], [], []
    for r in range(per_group):
        home = adapter_home[adapter_of[r]]
        owner = home // store_count
        picks.append(home - owner * store_count)
        place = jnp.int32(0)
        for o in owners:
            place = place + (o == owner).astype(jnp.int32)
        owners.append(owner)
        targets.append(owner * block + place * steps)
    col = lax.broadcasted_iota(jnp.int32, (sent_rows, own_rows), 1)
    row = lax.broadcasted_iota(jnp.int32, (sent_rows, own_rows), 0)
    want = jnp.zeros((sent_rows, own_rows), jnp.int32)
    mrow = lax.broadcasted_iota(jnp.int32, (own_rows, lanes), 0) // steps
    mlane = lax.broadcasted_iota(jnp.int32, (own_rows, lanes), 1) // rank
    mpick = jnp.zeros((own_rows, lanes), jnp.int32)
    for r in range(per_group):
        want = jnp.where(col // steps == r, targets[r] + lax.rem(col, steps), want)
        mpick = jnp.where(mrow == r, picks[r], mpick)
    pick_by_owner = (row == want).astype(f32).astype(bf16)
    mask = (mlane == mpick).astype(f32).astype(bf16)

    def flat(ref):
        for r in range(per_group):
            wide[r * steps : (r + 1) * steps] = ref[r].astype(f32)
        return wide[...].astype(bf16)

    h_out = jnp.dot(pick_by_owner, flat(hidden), preferred_element_type=f32)
    m_out = jnp.dot(pick_by_owner, mask, preferred_element_type=f32)
    h_send[:, :, :width] = h_out.reshape(groups, block, width).astype(bf16)
    h_send[:, :, width:] = m_out.reshape(groups, block, lanes).astype(bf16)
    mi = lax.broadcasted_iota(jnp.int32, (8, 128), 0)
    mj = lax.broadcasted_iota(jnp.int32, (8, 128), 1)
    meta = jnp.zeros((8, 128), jnp.int32)
    for r in range(per_group):
        meta = jnp.where((mi == 0) & (mj == r), new_group[r], meta)
        meta = jnp.where((mi == 1) & (mj == r), cached_len[r], meta)
    meta_send[...] = meta

    pl.semaphore_wait(barrier, groups - 1 + mps - 1)

    def copies(src, dst, ss, rs):
        out = {}
        for d in range(1, groups):
            out[d] = pltpu.make_async_remote_copy(
                src_ref=src(d),
                dst_ref=dst,
                send_sem=ss.at[d - 1],
                recv_sem=rs.at[d - 1],
                device_id=send_to(d),
                device_id_type=MESH,
            )
        return out

    h_cp = copies(lambda d: h_send.at[peer(d)], h_all.at[me], h_ss, h_rs)
    order = sorted(range(1, groups), key=lambda d: -min(d, groups - d))
    for d in order:
        h_cp[d].start()
    h_all[me] = h_send[me]

    fetch[6].wait()
    f_out = jnp.dot(pick_by_owner, flat(frozen), preferred_element_type=f32)
    f_send[...] = f_out.reshape(groups, block, width).astype(bf16)
    f_cp = copies(lambda d: f_send.at[peer(d)], f_all.at[me], f_ss, f_rs)
    for d in order:
        f_cp[d].start()
    f_all[me] = f_send[me]
    m_cp = copies(lambda d: meta_send, meta_all.at[me], m_ss, m_rs)
    for d in order:
        m_cp[d].start()
    meta_all[me] = meta

    fetch[8].wait()
    p_cp = {}
    for d in order:
        dest = peer(d)
        count = jnp.int32(0)
        sources = [jnp.int32(0)] * move_cap
        for r in range(per_group):
            hit = new_group[r] == dest
            for k in range(move_cap):
                sources[k] = jnp.where(hit & (count == k), r, sources[k])
            count = count + hit.astype(jnp.int32)
        for k in range(move_cap):
            slot = (d - 1) * move_cap + k
            for j in range(pages):
                page_id = page_table[sources[k], j]
                page_send[slot, :, pl.ds(j * page, page), :] = pool[:, page_id]
            p_cp[slot] = pltpu.make_async_remote_copy(
                src_ref=page_send.at[slot],
                dst_ref=rows.at[per_group + slot],
                send_sem=p_ss.at[slot],
                recv_sem=p_rs.at[slot],
                device_id=send_to(d),
                device_id_type=MESH,
            )

    def send_pages(k):
        for d in order:
            p_cp[(d - 1) * move_cap + k].start()

    send_pages(0)

    fetch[9].wait()
    for d in range(1, groups):
        h_cp[d].wait_recv()
    h_in = h_all[...].astype(f32).reshape(sent_rows, width + lanes)
    part = lax.dot_general(
        h_in[:, :width].astype(bf16),
        a_panels[...],
        (((1,), (1,)), ((), ())),
        preferred_element_type=f32,
    )
    r_part[...] = part * h_in[:, width:]
    r_cp = {}
    for d in range(1, mps):
        r_cp[d] = pltpu.make_async_remote_copy(
            src_ref=r_part,
            dst_ref=r_all.at[mp],
            send_sem=r_ss.at[d - 1],
            recv_sem=r_rs.at[d - 1],
            device_id=(rep, me, lax.rem(mp + d, mps)),
            device_id_type=MESH,
        )
        r_cp[d].start()
    r_all[mp] = r_part[...]

    @pl.loop(0, per_group)
    def _(r):
        for j in range(pages):
            rows[r, :, pl.ds(j * page, page), :] = pool[:, page_table[r, j]]

    for d in range(1, mps):
        r_cp[d].wait_recv()
    total = r_all[0]
    for j in range(1, mps):
        total = total + r_all[j]
    fetch[10].wait()
    for d in range(1, groups):
        f_cp[d].wait_recv()
    delta = jnp.dot(total.astype(bf16), b_panels[...], preferred_element_type=f32)
    q_done = f_all[...].astype(f32) + delta.reshape(groups, block, width)
    q_send[...] = q_done.astype(bf16)
    q_cp = copies(lambda d: q_send.at[peer(d)], q_all.at[me], q_ss, q_rs)
    for d in order:
        q_cp[d].start()
    for k in range(1, move_cap):
        send_pages(k)
    q_all[me] = q_send[me]
    fetch[7].wait()

    for d in range(1, groups):
        m_cp[d].wait_recv()
    local = pltpu.make_async_copy(meta_all, meta_s, l_sem)
    local.start()
    local.wait()
    entry_slot = [jnp.int32(r) for r in range(per_group)]
    entry_len = [cached_len[r] for r in range(per_group)]
    source = [jnp.int32(r) for r in range(per_group)]
    for d in range(1, groups):
        origin = lax.rem(me + groups - d, groups)
        count = jnp.int32(0)
        slots = [jnp.int32(0)] * move_cap
        for r in range(per_group):
            hit = meta_s[origin, 0, r] == me
            for k in range(move_cap):
                slots[k] = jnp.where(hit & (count == k), r, slots[k])
            source[r] = jnp.where(
                hit,
                per_group + (d - 1) * move_cap + jnp.minimum(count, move_cap - 1),
                source[r],
            )
            count = count + hit.astype(jnp.int32)
        for k in range(move_cap):
            entry_slot.append(slots[k])
            entry_len.append(meta_s[origin, 1, slots[k]])

    for d in range(1, groups):
        q_cp[d].wait_recv()
    q_in = q_all[...].astype(f32).reshape(sent_rows, width)
    qr = per_kv * steps
    ri = lax.broadcasted_iota(jnp.int32, (qr, per_kv * sent_rows), 0)
    ci = lax.broadcasted_iota(jnp.int32, (qr, per_kv * sent_rows), 1)
    base = ci - (ri // steps) * sent_rows - lax.rem(ri, steps)
    place = jnp.concatenate(
        [(base == targets[r]).astype(f32) for r in range(per_group)], axis=0
    ).astype(bf16)
    for h in range(kv_heads):
        stack = jnp.concatenate(
            [
                q_in[:, (h * per_kv + i) * HEAD : (h * per_kv + i + 1) * HEAD]
                for i in range(per_kv)
            ],
            axis=0,
        ).astype(bf16)
        got = jnp.dot(place, stack, preferred_element_type=f32)
        q_rows[:, h] = got.reshape(per_group, qr, HEAD).astype(bf16)

    scale = HEAD ** (-0.5)
    position = lax.broadcasted_iota(jnp.int32, (qr, context), 1)

    def attend(items):
        work = []
        for entry, slot, length in items:
            new = [fresh[slot, t].astype(f32) for t in range(steps)]
            for h in range(kv_heads):
                cols = slice(h * HEAD, (h + 1) * HEAD)
                q = q_rows[slot, h]
                s = lax.dot_general(
                    q, rows[entry, 0, :, cols], (((1,), (1,)), ((), ())), preferred_element_type=f32
                )
                s = jnp.where(position < length, s * scale, NEG_FILL)
                qf = q.astype(f32)
                extra = [
                    jnp.sum(qf * new[t][0:1, cols], axis=1, keepdims=True)
                    for t in range(steps)
                ]
                work.append((entry, h, cols, new, s, extra))
        scores = jnp.concatenate([w[4] for w in work], axis=0)
        extra = [jnp.concatenate([w[5][t] for w in work], axis=0) * scale for t in range(steps)]
        step_of = lax.rem(
            lax.broadcasted_iota(jnp.int32, (len(work) * qr, 1), 0), steps
        )
        extra = [jnp.where(step_of >= t, extra[t], NEG_FILL) for t in range(steps)]
        top = jnp.max(scores, axis=1, keepdims=True)
        for e in extra:
            top = jnp.maximum(top, e)
        weights = jnp.exp(scores - top)
        extra = [jnp.exp(e - top) for e in extra]
        norm = jnp.sum(weights, axis=1, keepdims=True)
        for e in extra:
            norm = norm + e
        prob = (weights / norm).astype(bf16)
        extra = [(e / norm).astype(bf16).astype(f32) for e in extra]
        for n, (entry, h, cols, new, _, _) in enumerate(work):
            part = slice(n * qr, (n + 1) * qr)
            o = jnp.dot(prob[part], rows[entry, 1, :, cols], preferred_element_type=f32)
            for t in range(steps):
                o = o + extra[t][part] * new[t][1:2, cols]
            att[entry, h] = o.astype(bf16)

    for r in range(0, per_group, 4):
        attend([(e, e, entry_len[e]) for e in range(r, min(r + 4, per_group))])
    near = sorted(range(1, groups), key=lambda d: min(d, groups - d))
    for k in range(move_cap):
        for n in range(0, len(near), 3):
            items = []
            for d in near[n : n + 3]:
                p_cp[(d - 1) * move_cap + k].wait_recv()
                e = per_group + (d - 1) * move_cap + k
                items.append((e, entry_slot[e], entry_len[e]))
            attend(items)

    for r in range(per_group):
        cache_out[:, r] = rows[source[r]]
    pr = lax.broadcasted_iota(jnp.int32, (per_kv * own_rows, per_group * qr), 0)
    pc = lax.broadcasted_iota(jnp.int32, (per_kv * own_rows, per_group * qr), 1)
    in_row = lax.rem(pr, own_rows)
    spread = (
        pc == (in_row // steps) * qr + (pr // own_rows) * steps + lax.rem(in_row, steps)
    )
    spread = spread.astype(f32).astype(bf16)
    for h in range(kv_heads):
        stack = jnp.concatenate([att[source[r], h] for r in range(per_group)], axis=0)
        got = jnp.dot(spread, stack, preferred_element_type=f32).astype(bf16)
        for i in range(per_kv):
            att_out[:, (h * per_kv + i) * HEAD : (h * per_kv + i + 1) * HEAD] = got[
                i * own_rows : (i + 1) * own_rows
            ]

    for d in range(1, groups):
        h_cp[d].wait_send()
        f_cp[d].wait_send()
        m_cp[d].wait_send()
        q_cp[d].wait_send()
    for d in range(1, mps):
        r_cp[d].wait_send()
    for slot in p_cp:
        p_cp[slot].wait_send()


def per_device(
    hidden_in,
    frozen_query_rows,
    new_kv,
    adapter_of,
    adapter_home,
    a_store,
    b_store,
    kv_pool,
    page_table,
    cached_len,
    new_group,
):
    groups = lax.axis_size("req")
    mps = lax.axis_size("mp")
    per_group, steps, width = hidden_in.shape
    store_count, rank, _ = a_store.shape
    pages, page = page_table.shape[1], kv_pool.shape[2]
    kv_width = kv_pool.shape[3]
    context = pages * page
    move_cap = -(-(per_group - per_group // 4) // groups)
    cap = -(-per_group // min(16, groups))
    block = -(-cap * steps // 8) * 8
    lanes = store_count * rank
    qr = width // kv_width * steps
    kv_heads = kv_width // HEAD
    moved = (groups - 1) * move_cap
    entries = per_group + moved
    bf16, f32 = jnp.bfloat16, jnp.float32
    cfg = (groups, mps, per_group, steps, cap, block, store_count, rank, pages, page, move_cap)
    dma = pltpu.SemaphoreType.DMA
    given = (
        adapter_of,
        adapter_home,
        page_table,
        cached_len,
        new_group,
        hidden_in,
        frozen_query_rows,
        new_kv,
        kv_pool,
        a_store.reshape(lanes, width),
        b_store.reshape(lanes, width),
    )
    att, cache = pl.pallas_call(
        functools.partial(kernel, cfg),
        out_shape=(
            jax.ShapeDtypeStruct((per_group * steps, width), bf16),
            jax.ShapeDtypeStruct((2, per_group, context, kv_width), bf16),
        ),
        in_specs=[pl.BlockSpec(memory_space=pltpu.HBM)] * len(given),
        out_specs=[pl.BlockSpec(memory_space=VMEM)] * 2,
        scratch_shapes=[SMEM(g.shape, g.dtype) for g in given[:5]]
        + [VMEM(g.shape, g.dtype) for g in given[5:]]
        + [
            dma((len(given),)),
            VMEM((groups, block, width + lanes), bf16),
            VMEM((groups, block, width + lanes), bf16),
            VMEM((groups, block, width), bf16),
            VMEM((groups, block, width), bf16),
            VMEM((groups * block, lanes), f32),
            VMEM((mps, groups * block, lanes), f32),
            VMEM((groups, block, width), bf16),
            VMEM((groups, block, width), bf16),
            VMEM((per_group, kv_heads, qr, HEAD), bf16),
            VMEM((per_group * steps, width), f32),
            VMEM((8, 128), jnp.int32),
            VMEM((groups, 8, 128), jnp.int32),
            SMEM((groups, 8, 128), jnp.int32),
            VMEM((moved, 2, context, kv_width), bf16),
            VMEM((entries, 2, context, kv_width), bf16),
            VMEM((entries, kv_heads, qr, HEAD), bf16),
            dma((groups - 1,)),
            dma((groups - 1,)),
            dma((groups - 1,)),
            dma((groups - 1,)),
            dma((mps - 1,)),
            dma((mps - 1,)),
            dma((groups - 1,)),
            dma((groups - 1,)),
            dma((groups - 1,)),
            dma((groups - 1,)),
            dma((moved,)),
            dma((moved,)),
            dma,
        ],
        compiler_params=pltpu.CompilerParams(
            collective_id=0, has_side_effects=True, vmem_limit_bytes=62 * 2**20
        ),
    )(*given)
    return att.reshape(per_group, steps, width), cache


def solution(mesh):
    placed = (
        P(("rep", "req"), None, "mp"),
        P(("rep", "req"), None, "mp"),
        P(("rep", "req"), None, None, "mp"),
        P(("rep", "req")),
        P("rep"),
        P(("rep", "req"), None, "mp"),
        P(("rep", "req"), None, "mp"),
        P(None, ("rep", "req"), None, "mp"),
        P(("rep", "req"), None),
        P(("rep", "req")),
        P(("rep", "req")),
    )
    return jax.shard_map(
        per_device,
        mesh=mesh,
        in_specs=placed,
        out_specs=(P(("rep", "req"), None, "mp"), P(None, ("rep", "req"), None, "mp")),
        check_vma=False,
    )
```

```python
import functools

import jax
import jax.numpy as jnp
from jax import lax
from jax.experimental import pallas as pl
from jax.experimental.pallas import tpu as pltpu
from jax.sharding import PartitionSpec as P

HEAD = 128
NEG_FILL = -1e30
MESH = pl.DeviceIdType.MESH
VMEM = pltpu.VMEM
SMEM = pltpu.SMEM


def kernel(
    cfg,
    *refs,
):
    given, refs = refs[:11], refs[11:]
    body(cfg, given, refs[2:13], refs[13], *refs[:2], *refs[14:])


def body(
    cfg,
    given,
    held,
    in_sem,
    att_out,
    cache_out,
    h_send,
    h_all,
    f_send,
    f_all,
    r_part,
    r_all,
    q_send,
    q_all,
    q_rows,
    wide,
    meta_send,
    meta_all,
    meta_s,
    page_send,
    rows,
    att,
    h_ss,
    h_rs,
    f_ss,
    f_rs,
    r_ss,
    r_rs,
    q_ss,
    q_rs,
    m_ss,
    m_rs,
    p_ss,
    p_rs,
    l_sem,
):
    groups, mps, per_group, steps, cap, block, store_count, rank, pages, page, move_cap = cfg
    f32, bf16 = jnp.float32, jnp.bfloat16
    rep = lax.axis_index("rep")
    me = lax.axis_index("req")
    mp = lax.axis_index("mp")
    fetch = [
        pltpu.make_async_copy(src, dst, in_sem.at[i])
        for i, (src, dst) in enumerate(zip(given, held))
    ]
    for f in fetch:
        f.start()
    (
        adapter_of,
        adapter_home,
        page_table,
        cached_len,
        new_group,
        hidden,
        frozen,
        fresh,
        pool,
        a_panels,
        b_panels,
    ) = held
    width = hidden.shape[2]
    lanes = store_count * rank
    kv_width = pool.shape[3]
    kv_heads = kv_width // HEAD
    per_kv = width // kv_width
    context = pages * page
    sent_rows = groups * block
    own_rows = per_group * steps

    def peer(d):
        return lax.rem(me + d, groups)

    def send_to(d):
        return (rep, peer(d), mp)

    barrier = pltpu.get_barrier_semaphore()
    for d in range(1, groups):
        pl.semaphore_signal(barrier, inc=1, device_id=send_to(d), device_id_type=MESH)
    for d in range(1, mps):
        pl.semaphore_signal(
            barrier, inc=1, device_id=(rep, me, lax.rem(mp + d, mps)), device_id_type=MESH
        )

    for f in fetch[:6]:
        f.wait()

    owners, picks, targets = [], [], []
    for r in range(per_group):
        home = adapter_home[adapter_of[r]]
        owner = home // store_count
        picks.append(home - owner * store_count)
        place = jnp.int32(0)
        for o in owners:
            place = place + (o == owner).astype(jnp.int32)
        owners.append(owner)
        targets.append(owner * block + place * steps)
    col = lax.broadcasted_iota(jnp.int32, (sent_rows, own_rows), 1)
    row = lax.broadcasted_iota(jnp.int32, (sent_rows, own_rows), 0)
    want = jnp.zeros((sent_rows, own_rows), jnp.int32)
    mrow = lax.broadcasted_iota(jnp.int32, (own_rows, lanes), 0) // steps
    mlane = lax.broadcasted_iota(jnp.int32, (own_rows, lanes), 1) // rank
    mpick = jnp.zeros((own_rows, lanes), jnp.int32)
    for r in range(per_group):
        want = jnp.where(col // steps == r, targets[r] + lax.rem(col, steps), want)
        mpick = jnp.where(mrow == r, picks[r], mpick)
    pick_by_owner = (row == want).astype(f32).astype(bf16)
    mask = (mlane == mpick).astype(f32).astype(bf16)

    def flat(ref):
        for r in range(per_group):
            wide[r * steps : (r + 1) * steps] = ref[r].astype(f32)
        return wide[...].astype(bf16)

    h_out = jnp.dot(pick_by_owner, flat(hidden), preferred_element_type=f32)
    m_out = jnp.dot(pick_by_owner, mask, preferred_element_type=f32)
    h_send[:, :, :width] = h_out.reshape(groups, block, width).astype(bf16)
    h_send[:, :, width:] = m_out.reshape(groups, block, lanes).astype(bf16)
    mi = lax.broadcasted_iota(jnp.int32, (8, 128), 0)
    mj = lax.broadcasted_iota(jnp.int32, (8, 128), 1)
    meta = jnp.zeros((8, 128), jnp.int32)
    for r in range(per_group):
        meta = jnp.where((mi == 0) & (mj == r), new_group[r], meta)
        meta = jnp.where((mi == 1) & (mj == r), cached_len[r], meta)
    meta_send[...] = meta

    pl.semaphore_wait(barrier, groups - 1 + mps - 1)

    def copies(src, dst, ss, rs):
        out = {}
        for d in range(1, groups):
            out[d] = pltpu.make_async_remote_copy(
                src_ref=src(d),
                dst_ref=dst,
                send_sem=ss.at[d - 1],
                recv_sem=rs.at[d - 1],
                device_id=send_to(d),
                device_id_type=MESH,
            )
        return out

    h_cp = copies(lambda d: h_send.at[peer(d)], h_all.at[me], h_ss, h_rs)
    order = sorted(range(1, groups), key=lambda d: -min(d, groups - d))
    for d in order:
        h_cp[d].start()
    h_all[me] = h_send[me]

    fetch[6].wait()
    f_out = jnp.dot(pick_by_owner, flat(frozen), preferred_element_type=f32)
    f_send[...] = f_out.reshape(groups, block, width).astype(bf16)
    f_cp = copies(lambda d: f_send.at[peer(d)], f_all.at[me], f_ss, f_rs)
    for d in order:
        f_cp[d].start()
    f_all[me] = f_send[me]
    m_cp = copies(lambda d: meta_send, meta_all.at[me], m_ss, m_rs)
    for d in order:
        m_cp[d].start()
    meta_all[me] = meta

    fetch[8].wait()
    p_cp = {}
    for d in order:
        dest = peer(d)
        count = jnp.int32(0)
        sources = [jnp.int32(0)] * move_cap
        for r in range(per_group):
            hit = new_group[r] == dest
            for k in range(move_cap):
                sources[k] = jnp.where(hit & (count == k), r, sources[k])
            count = count + hit.astype(jnp.int32)
        for k in range(move_cap):
            slot = (d - 1) * move_cap + k
            for j in range(pages):
                page_id = page_table[j, sources[k]]
                page_send[slot, :, pl.ds(j * page, page), :] = pool[:, page_id]
            p_cp[slot] = pltpu.make_async_remote_copy(
                src_ref=page_send.at[slot],
                dst_ref=rows.at[per_group + slot],
                send_sem=p_ss.at[slot],
                recv_sem=p_rs.at[slot],
                device_id=send_to(d),
                device_id_type=MESH,
            )

    def send_pages(k):
        for d in order:
            p_cp[(d - 1) * move_cap + k].start()

    send_pages(0)

    fetch[9].wait()
    for d in range(1, groups):
        h_cp[d].wait_recv()
    h_in = h_all[...].astype(f32).reshape(sent_rows, width + lanes)
    part = lax.dot_general(
        h_in[:, :width].astype(bf16),
        a_panels[...],
        (((1,), (1,)), ((), ())),
        preferred_element_type=f32,
    )
    r_part[...] = part * h_in[:, width:]
    r_cp = {}
    for d in range(1, mps):
        r_cp[d] = pltpu.make_async_remote_copy(
            src_ref=r_part,
            dst_ref=r_all.at[mp],
            send_sem=r_ss.at[d - 1],
            recv_sem=r_rs.at[d - 1],
            device_id=(rep, me, lax.rem(mp + d, mps)),
            device_id_type=MESH,
        )
        r_cp[d].start()
    r_all[mp] = r_part[...]

    @pl.loop(0, per_group)
    def _(r):
        for j in range(pages):
            rows[r, :, pl.ds(j * page, page), :] = pool[:, page_table[j, r]]

    for d in range(1, mps):
        r_cp[d].wait_recv()
    total = r_all[0]
    for j in range(1, mps):
        total = total + r_all[j]
    fetch[10].wait()
    for d in range(1, groups):
        f_cp[d].wait_recv()
    delta = jnp.dot(total.astype(bf16), b_panels[...], preferred_element_type=f32)
    q_done = f_all[...].astype(f32) + delta.reshape(groups, block, width)
    q_send[...] = q_done.astype(bf16)
    q_cp = copies(lambda d: q_send.at[peer(d)], q_all.at[me], q_ss, q_rs)
    for d in order:
        q_cp[d].start()
    for k in range(1, move_cap):
        send_pages(k)
    q_all[me] = q_send[me]
    fetch[7].wait()

    for d in range(1, groups):
        m_cp[d].wait_recv()
    local = pltpu.make_async_copy(meta_all, meta_s, l_sem)
    local.start()
    local.wait()
    entry_slot = [jnp.int32(r) for r in range(per_group)]
    entry_len = [cached_len[r] for r in range(per_group)]
    source = [jnp.int32(r) for r in range(per_group)]
    for d in range(1, groups):
        origin = lax.rem(me + groups - d, groups)
        count = jnp.int32(0)
        slots = [jnp.int32(0)] * move_cap
        for r in range(per_group):
            hit = meta_s[origin, 0, r] == me
            for k in range(move_cap):
                slots[k] = jnp.where(hit & (count == k), r, slots[k])
            source[r] = jnp.where(
                hit,
                per_group + (d - 1) * move_cap + jnp.minimum(count, move_cap - 1),
                source[r],
            )
            count = count + hit.astype(jnp.int32)
        for k in range(move_cap):
            entry_slot.append(slots[k])
            entry_len.append(meta_s[origin, 1, slots[k]])

    for d in range(1, groups):
        q_cp[d].wait_recv()
    q_in = q_all[...].astype(f32).reshape(sent_rows, width)
    qr = per_kv * steps
    ri = lax.broadcasted_iota(jnp.int32, (qr, per_kv * sent_rows), 0)
    ci = lax.broadcasted_iota(jnp.int32, (qr, per_kv * sent_rows), 1)
    base = ci - (ri // steps) * sent_rows - lax.rem(ri, steps)
    place = jnp.concatenate(
        [(base == targets[r]).astype(f32) for r in range(per_group)], axis=0
    ).astype(bf16)
    for h in range(kv_heads):
        stack = jnp.concatenate(
            [
                q_in[:, (h * per_kv + i) * HEAD : (h * per_kv + i + 1) * HEAD]
                for i in range(per_kv)
            ],
            axis=0,
        ).astype(bf16)
        got = jnp.dot(place, stack, preferred_element_type=f32)
        q_rows[:, h] = got.reshape(per_group, qr, HEAD).astype(bf16)

    scale = HEAD ** (-0.5)
    position = lax.broadcasted_iota(jnp.int32, (qr, context), 1)

    def attend(items):
        work = []
        for entry, slot, length in items:
            new = [fresh[slot, t].astype(f32) for t in range(steps)]
            for h in range(kv_heads):
                cols = slice(h * HEAD, (h + 1) * HEAD)
                q = q_rows[slot, h]
                s = lax.dot_general(
                    q, rows[entry, 0, :, cols], (((1,), (1,)), ((), ())), preferred_element_type=f32
                )
                s = jnp.where(position < length, s * scale, NEG_FILL)
                qf = q.astype(f32)
                extra = [
                    jnp.sum(qf * new[t][0:1, cols], axis=1, keepdims=True)
                    for t in range(steps)
                ]
                work.append((entry, h, cols, new, s, extra))
        scores = jnp.concatenate([w[4] for w in work], axis=0)
        extra = [jnp.concatenate([w[5][t] for w in work], axis=0) * scale for t in range(steps)]
        step_of = lax.rem(
            lax.broadcasted_iota(jnp.int32, (len(work) * qr, 1), 0), steps
        )
        extra = [jnp.where(step_of >= t, extra[t], NEG_FILL) for t in range(steps)]
        top = jnp.max(scores, axis=1, keepdims=True)
        for e in extra:
            top = jnp.maximum(top, e)
        weights = jnp.exp(scores - top)
        extra = [jnp.exp(e - top) for e in extra]
        norm = jnp.sum(weights, axis=1, keepdims=True)
        for e in extra:
            norm = norm + e
        prob = (weights / norm).astype(bf16)
        extra = [(e / norm).astype(bf16).astype(f32) for e in extra]
        for n, (entry, h, cols, new, _, _) in enumerate(work):
            part = slice(n * qr, (n + 1) * qr)
            o = jnp.dot(prob[part], rows[entry, 1, :, cols], preferred_element_type=f32)
            for t in range(steps):
                o = o + extra[t][part] * new[t][1:2, cols]
            att[entry, h] = o.astype(bf16)

    for r in range(0, per_group, 4):
        attend([(e, e, entry_len[e]) for e in range(r, min(r + 4, per_group))])
    near = sorted(range(1, groups), key=lambda d: min(d, groups - d))
    for k in range(move_cap):
        for n in range(0, len(near), 3):
            items = []
            for d in near[n : n + 3]:
                p_cp[(d - 1) * move_cap + k].wait_recv()
                e = per_group + (d - 1) * move_cap + k
                items.append((e, entry_slot[e], entry_len[e]))
            attend(items)

    for r in range(per_group):
        cache_out[:, r] = rows[source[r]]
    pr = lax.broadcasted_iota(jnp.int32, (per_kv * own_rows, per_group * qr), 0)
    pc = lax.broadcasted_iota(jnp.int32, (per_kv * own_rows, per_group * qr), 1)
    in_row = lax.rem(pr, own_rows)
    spread = (
        pc == (in_row // steps) * qr + (pr // own_rows) * steps + lax.rem(in_row, steps)
    )
    spread = spread.astype(f32).astype(bf16)
    for h in range(kv_heads):
        stack = jnp.concatenate([att[source[r], h] for r in range(per_group)], axis=0)
        got = jnp.dot(spread, stack, preferred_element_type=f32).astype(bf16)
        for i in range(per_kv):
            att_out[:, (h * per_kv + i) * HEAD : (h * per_kv + i + 1) * HEAD] = got[
                i * own_rows : (i + 1) * own_rows
            ]

    for d in range(1, groups):
        h_cp[d].wait_send()
        f_cp[d].wait_send()
        m_cp[d].wait_send()
        q_cp[d].wait_send()
    for d in range(1, mps):
        r_cp[d].wait_send()
    for slot in p_cp:
        p_cp[slot].wait_send()


def per_device(
    hidden_in,
    frozen_query_rows,
    new_kv,
    adapter_of,
    adapter_home,
    a_store,
    b_store,
    kv_pool,
    page_table,
    cached_len,
    new_group,
):
    groups = lax.axis_size("req")
    mps = lax.axis_size("mp")
    per_group, steps, width = hidden_in.shape
    store_count, rank, _ = a_store.shape
    pages, page = page_table.shape[1], kv_pool.shape[2]
    kv_width = kv_pool.shape[3]
    context = pages * page
    move_cap = -(-(per_group - per_group // 4) // groups)
    cap = -(-per_group // min(16, groups))
    block = -(-cap * steps // 8) * 8
    lanes = store_count * rank
    qr = width // kv_width * steps
    kv_heads = kv_width // HEAD
    moved = (groups - 1) * move_cap
    entries = per_group + moved
    bf16, f32 = jnp.bfloat16, jnp.float32
    cfg = (groups, mps, per_group, steps, cap, block, store_count, rank, pages, page, move_cap)
    dma = pltpu.SemaphoreType.DMA
    given = (
        adapter_of,
        adapter_home,
        page_table.T,
        cached_len,
        new_group,
        hidden_in,
        frozen_query_rows,
        new_kv,
        kv_pool,
        a_store.reshape(lanes, width),
        b_store.reshape(lanes, width),
    )
    att, cache = pl.pallas_call(
        functools.partial(kernel, cfg),
        out_shape=(
            jax.ShapeDtypeStruct((per_group * steps, width), bf16),
            jax.ShapeDtypeStruct((2, per_group, context, kv_width), bf16),
        ),
        in_specs=[pl.BlockSpec(memory_space=pltpu.HBM)] * len(given),
        out_specs=[pl.BlockSpec(memory_space=VMEM)] * 2,
        scratch_shapes=[SMEM(g.shape, g.dtype) for g in given[:5]]
        + [VMEM(g.shape, g.dtype) for g in given[5:]]
        + [
            dma((len(given),)),
            VMEM((groups, block, width + lanes), bf16),
            VMEM((groups, block, width + lanes), bf16),
            VMEM((groups, block, width), bf16),
            VMEM((groups, block, width), bf16),
            VMEM((groups * block, lanes), f32),
            VMEM((mps, groups * block, lanes), f32),
            VMEM((groups, block, width), bf16),
            VMEM((groups, block, width), bf16),
            VMEM((per_group, kv_heads, qr, HEAD), bf16),
            VMEM((per_group * steps, width), f32),
            VMEM((8, 128), jnp.int32),
            VMEM((groups, 8, 128), jnp.int32),
            SMEM((groups, 8, 128), jnp.int32),
            VMEM((moved, 2, context, kv_width), bf16),
            VMEM((entries, 2, context, kv_width), bf16),
            VMEM((entries, kv_heads, qr, HEAD), bf16),
            dma((groups - 1,)),
            dma((groups - 1,)),
            dma((groups - 1,)),
            dma((groups - 1,)),
            dma((mps - 1,)),
            dma((mps - 1,)),
            dma((groups - 1,)),
            dma((groups - 1,)),
            dma((groups - 1,)),
            dma((groups - 1,)),
            dma((moved,)),
            dma((moved,)),
            dma,
        ],
        compiler_params=pltpu.CompilerParams(
            collective_id=0, has_side_effects=True, vmem_limit_bytes=40 * 2**20
        ),
    )(*[pltpu.with_memory_space_constraint(g, pltpu.HBM) for g in given])
    return att.reshape(per_group, steps, width), cache


def solution(mesh):
    placed = (
        P(("rep", "req"), None, "mp"),
        P(("rep", "req"), None, "mp"),
        P(("rep", "req"), None, None, "mp"),
        P(("rep", "req")),
        P("rep"),
        P(("rep", "req"), None, "mp"),
        P(("rep", "req"), None, "mp"),
        P(None, ("rep", "req"), None, "mp"),
        P(("rep", "req"), None),
        P(("rep", "req")),
        P(("rep", "req")),
    )
    return jax.shard_map(
        per_device,
        mesh=mesh,
        in_specs=placed,
        out_specs=(P(("rep", "req"), None, "mp"), P(None, ("rep", "req"), None, "mp")),
        check_vma=False,
    )
```

```python
import functools

import jax
import jax.numpy as jnp
from jax import lax
from jax.experimental import pallas as pl
from jax.experimental.pallas import tpu as pltpu
from jax.sharding import PartitionSpec as P

HEAD = 128
NEG_FILL = -1e30
MESH = pl.DeviceIdType.MESH
VMEM = pltpu.VMEM
SMEM = pltpu.SMEM


def kernel(
    cfg,
    *refs,
):
    given, refs = refs[:11], refs[11:]
    body(cfg, given, refs[2:13], refs[13], *refs[:2], *refs[14:])


def body(
    cfg,
    given,
    held,
    in_sem,
    att_out,
    cache_out,
    h_send,
    h_all,
    f_send,
    f_all,
    r_part,
    r_all,
    q_send,
    q_all,
    q_rows,
    wide,
    meta_send,
    meta_all,
    meta_s,
    page_send,
    rows,
    att,
    h_ss,
    h_rs,
    f_ss,
    f_rs,
    r_ss,
    r_rs,
    q_ss,
    q_rs,
    m_ss,
    m_rs,
    p_ss,
    p_rs,
    l_sem,
):
    groups, mps, per_group, steps, cap, block, store_count, rank, pages, page, move_cap = cfg
    f32, bf16 = jnp.float32, jnp.bfloat16
    rep = lax.axis_index("rep")
    me = lax.axis_index("req")
    mp = lax.axis_index("mp")
    fetch = [
        pltpu.make_async_copy(src, dst, in_sem.at[i])
        for i, (src, dst) in enumerate(zip(given, held))
    ]
    for f in fetch:
        f.start()
    (
        adapter_of,
        adapter_home,
        page_table,
        cached_len,
        new_group,
        hidden,
        frozen,
        fresh,
        pool,
        a_panels,
        b_panels,
    ) = held
    width = hidden.shape[2]
    lanes = store_count * rank
    kv_width = pool.shape[3]
    kv_heads = kv_width // HEAD
    per_kv = width // kv_width
    context = pages * page
    sent_rows = groups * block
    own_rows = per_group * steps

    def peer(d):
        return lax.rem(me + d, groups)

    def send_to(d):
        return (rep, peer(d), mp)

    barrier = pltpu.get_barrier_semaphore()
    for d in range(1, groups):
        pl.semaphore_signal(barrier, inc=1, device_id=send_to(d), device_id_type=MESH)
    for d in range(1, mps):
        pl.semaphore_signal(
            barrier, inc=1, device_id=(rep, me, lax.rem(mp + d, mps)), device_id_type=MESH
        )

    for f in fetch[:6]:
        f.wait()

    owners, picks, targets = [], [], []
    for r in range(per_group):
        home = adapter_home[adapter_of[r]]
        owner = home // store_count
        picks.append(home - owner * store_count)
        place = jnp.int32(0)
        for o in owners:
            place = place + (o == owner).astype(jnp.int32)
        owners.append(owner)
        targets.append(owner * block + place * steps)
    col = lax.broadcasted_iota(jnp.int32, (sent_rows, own_rows), 1)
    row = lax.broadcasted_iota(jnp.int32, (sent_rows, own_rows), 0)
    want = jnp.zeros((sent_rows, own_rows), jnp.int32)
    mrow = lax.broadcasted_iota(jnp.int32, (own_rows, lanes), 0) // steps
    mlane = lax.broadcasted_iota(jnp.int32, (own_rows, lanes), 1) // rank
    mpick = jnp.zeros((own_rows, lanes), jnp.int32)
    for r in range(per_group):
        want = jnp.where(col // steps == r, targets[r] + lax.rem(col, steps), want)
        mpick = jnp.where(mrow == r, picks[r], mpick)
    pick_by_owner = (row == want).astype(f32).astype(bf16)
    mask = (mlane == mpick).astype(f32).astype(bf16)

    def flat(ref):
        for r in range(per_group):
            wide[r * steps : (r + 1) * steps] = ref[r].astype(f32)
        return wide[...].astype(bf16)

    h_out = jnp.dot(pick_by_owner, flat(hidden), preferred_element_type=f32)
    m_out = jnp.dot(pick_by_owner, mask, preferred_element_type=f32)
    h_send[:, :, :width] = h_out.reshape(groups, block, width).astype(bf16)
    h_send[:, :, width:] = m_out.reshape(groups, block, lanes).astype(bf16)
    mi = lax.broadcasted_iota(jnp.int32, (8, 128), 0)
    mj = lax.broadcasted_iota(jnp.int32, (8, 128), 1)
    meta = jnp.zeros((8, 128), jnp.int32)
    for r in range(per_group):
        meta = jnp.where((mi == 0) & (mj == r), new_group[r], meta)
        meta = jnp.where((mi == 1) & (mj == r), cached_len[r], meta)
    meta_send[...] = meta

    pl.semaphore_wait(barrier, groups - 1 + mps - 1)

    def copies(src, dst, ss, rs):
        out = {}
        for d in range(1, groups):
            out[d] = pltpu.make_async_remote_copy(
                src_ref=src(d),
                dst_ref=dst,
                send_sem=ss.at[d - 1],
                recv_sem=rs.at[d - 1],
                device_id=send_to(d),
                device_id_type=MESH,
            )
        return out

    h_cp = copies(lambda d: h_send.at[peer(d)], h_all.at[me], h_ss, h_rs)
    order = sorted(range(1, groups), key=lambda d: -min(d, groups - d))
    for d in order:
        h_cp[d].start()
    h_all[me] = h_send[me]

    fetch[6].wait()
    f_out = jnp.dot(pick_by_owner, flat(frozen), preferred_element_type=f32)
    f_send[...] = f_out.reshape(groups, block, width).astype(bf16)
    f_cp = copies(lambda d: f_send.at[peer(d)], f_all.at[me], f_ss, f_rs)
    for d in order:
        f_cp[d].start()
    f_all[me] = f_send[me]
    m_cp = copies(lambda d: meta_send, meta_all.at[me], m_ss, m_rs)
    for d in order:
        m_cp[d].start()
    meta_all[me] = meta

    fetch[8].wait()
    p_cp, sources = {}, {}
    for d in order:
        dest = peer(d)
        count = jnp.int32(0)
        picked = [jnp.int32(0)] * move_cap
        for r in range(per_group):
            hit = new_group[r] == dest
            for k in range(move_cap):
                picked[k] = jnp.where(hit & (count == k), r, picked[k])
            count = count + hit.astype(jnp.int32)
        sources[d] = picked

    def pack_pages(k):
        for d in order:
            slot = (d - 1) * move_cap + k
            for j in range(pages):
                page_id = page_table[j, sources[d][k]]
                page_send[slot, :, pl.ds(j * page, page), :] = pool[:, page_id]
            p_cp[slot] = pltpu.make_async_remote_copy(
                src_ref=page_send.at[slot],
                dst_ref=rows.at[per_group + slot],
                send_sem=p_ss.at[slot],
                recv_sem=p_rs.at[slot],
                device_id=send_to(d),
                device_id_type=MESH,
            )
            if k == 0 or (k == 1 and d == order[0]):
                p_cp[slot].start()

    def send_pages(k):
        for d in order[1:] if k == 1 else order:
            p_cp[(d - 1) * move_cap + k].start()

    pack_pages(0)

    fetch[9].wait()
    for d in range(1, groups):
        h_cp[d].wait_recv()
    h_in = h_all[...].astype(f32).reshape(sent_rows, width + lanes)
    part = lax.dot_general(
        h_in[:, :width].astype(bf16),
        a_panels[...],
        (((1,), (1,)), ((), ())),
        preferred_element_type=f32,
    )
    r_part[...] = part * h_in[:, width:]
    r_cp = {}
    for d in range(1, mps):
        r_cp[d] = pltpu.make_async_remote_copy(
            src_ref=r_part,
            dst_ref=r_all.at[mp],
            send_sem=r_ss.at[d - 1],
            recv_sem=r_rs.at[d - 1],
            device_id=(rep, me, lax.rem(mp + d, mps)),
            device_id_type=MESH,
        )
        r_cp[d].start()
    r_all[mp] = r_part[...]

    for k in range(1, move_cap):
        pack_pages(k)

    @pl.loop(0, per_group)
    def _(r):
        for j in range(pages):
            rows[r, :, pl.ds(j * page, page), :] = pool[:, page_table[j, r]]

    for d in range(1, mps):
        r_cp[d].wait_recv()
    total = r_all[0]
    for j in range(1, mps):
        total = total + r_all[j]
    fetch[10].wait()
    for d in range(1, groups):
        f_cp[d].wait_recv()
    delta = jnp.dot(total.astype(bf16), b_panels[...], preferred_element_type=f32)
    q_done = f_all[...].astype(f32) + delta.reshape(groups, block, width)
    q_send[...] = q_done.astype(bf16)
    q_cp = copies(lambda d: q_send.at[peer(d)], q_all.at[me], q_ss, q_rs)
    for d in order:
        q_cp[d].start()
    for k in range(1, move_cap):
        send_pages(k)
    q_all[me] = q_send[me]
    fetch[7].wait()

    for d in range(1, groups):
        m_cp[d].wait_recv()
    local = pltpu.make_async_copy(meta_all, meta_s, l_sem)
    local.start()
    local.wait()
    entry_slot = [jnp.int32(r) for r in range(per_group)]
    entry_len = [cached_len[r] for r in range(per_group)]
    source = [jnp.int32(r) for r in range(per_group)]
    for d in range(1, groups):
        origin = lax.rem(me + groups - d, groups)
        count = jnp.int32(0)
        slots = [jnp.int32(0)] * move_cap
        for r in range(per_group):
            hit = meta_s[origin, 0, r] == me
            for k in range(move_cap):
                slots[k] = jnp.where(hit & (count == k), r, slots[k])
            source[r] = jnp.where(
                hit,
                per_group + (d - 1) * move_cap + jnp.minimum(count, move_cap - 1),
                source[r],
            )
            count = count + hit.astype(jnp.int32)
        for k in range(move_cap):
            entry_slot.append(slots[k])
            entry_len.append(meta_s[origin, 1, slots[k]])

    for d in range(1, groups):
        q_cp[d].wait_recv()
    q_in = q_all[...].astype(f32).reshape(sent_rows, width)
    qr = per_kv * steps
    ri = lax.broadcasted_iota(jnp.int32, (qr, per_kv * sent_rows), 0)
    ci = lax.broadcasted_iota(jnp.int32, (qr, per_kv * sent_rows), 1)
    base = ci - (ri // steps) * sent_rows - lax.rem(ri, steps)
    place = jnp.concatenate(
        [(base == targets[r]).astype(f32) for r in range(per_group)], axis=0
    ).astype(bf16)
    for h in range(kv_heads):
        stack = jnp.concatenate(
            [
                q_in[:, (h * per_kv + i) * HEAD : (h * per_kv + i + 1) * HEAD]
                for i in range(per_kv)
            ],
            axis=0,
        ).astype(bf16)
        got = jnp.dot(place, stack, preferred_element_type=f32)
        q_rows[:, h] = got.reshape(per_group, qr, HEAD).astype(bf16)

    scale = HEAD ** (-0.5)
    position = lax.broadcasted_iota(jnp.int32, (qr, context), 1)

    def attend(items):
        work = []
        for entry, slot, length in items:
            new = [fresh[slot, t].astype(f32) for t in range(steps)]
            for h in range(kv_heads):
                cols = slice(h * HEAD, (h + 1) * HEAD)
                q = q_rows[slot, h]
                s = lax.dot_general(
                    q, rows[entry, 0, :, cols], (((1,), (1,)), ((), ())), preferred_element_type=f32
                )
                s = jnp.where(position < length, s * scale, NEG_FILL)
                qf = q.astype(f32)
                extra = [
                    jnp.sum(qf * new[t][0:1, cols], axis=1, keepdims=True)
                    for t in range(steps)
                ]
                work.append((entry, h, cols, new, s, extra))
        scores = jnp.concatenate([w[4] for w in work], axis=0)
        extra = [jnp.concatenate([w[5][t] for w in work], axis=0) * scale for t in range(steps)]
        step_of = lax.rem(
            lax.broadcasted_iota(jnp.int32, (len(work) * qr, 1), 0), steps
        )
        extra = [jnp.where(step_of >= t, extra[t], NEG_FILL) for t in range(steps)]
        top = jnp.max(scores, axis=1, keepdims=True)
        for e in extra:
            top = jnp.maximum(top, e)
        weights = jnp.exp(scores - top)
        extra = [jnp.exp(e - top) for e in extra]
        norm = jnp.sum(weights, axis=1, keepdims=True)
        for e in extra:
            norm = norm + e
        prob = (weights / norm).astype(bf16)
        extra = [(e / norm).astype(bf16).astype(f32) for e in extra]
        for n, (entry, h, cols, new, _, _) in enumerate(work):
            part = slice(n * qr, (n + 1) * qr)
            o = jnp.dot(prob[part], rows[entry, 1, :, cols], preferred_element_type=f32)
            for t in range(steps):
                o = o + extra[t][part] * new[t][1:2, cols]
            att[entry, h] = o.astype(bf16)

    for r in range(0, per_group, 4):
        attend([(e, e, entry_len[e]) for e in range(r, min(r + 4, per_group))])
    near = sorted(range(1, groups), key=lambda d: min(d, groups - d))
    for k in range(move_cap):
        for n in range(0, len(near), 3):
            items = []
            for d in near[n : n + 3]:
                p_cp[(d - 1) * move_cap + k].wait_recv()
                e = per_group + (d - 1) * move_cap + k
                items.append((e, entry_slot[e], entry_len[e]))
            attend(items)

    for r in range(per_group):
        cache_out[:, r] = rows[source[r]]
    pr = lax.broadcasted_iota(jnp.int32, (per_kv * own_rows, per_group * qr), 0)
    pc = lax.broadcasted_iota(jnp.int32, (per_kv * own_rows, per_group * qr), 1)
    in_row = lax.rem(pr, own_rows)
    spread = (
        pc == (in_row // steps) * qr + (pr // own_rows) * steps + lax.rem(in_row, steps)
    )
    spread = spread.astype(f32).astype(bf16)
    for h in range(kv_heads):
        stack = jnp.concatenate([att[source[r], h] for r in range(per_group)], axis=0)
        got = jnp.dot(spread, stack, preferred_element_type=f32).astype(bf16)
        for i in range(per_kv):
            att_out[:, (h * per_kv + i) * HEAD : (h * per_kv + i + 1) * HEAD] = got[
                i * own_rows : (i + 1) * own_rows
            ]

    for d in range(1, groups):
        h_cp[d].wait_send()
        f_cp[d].wait_send()
        m_cp[d].wait_send()
        q_cp[d].wait_send()
    for d in range(1, mps):
        r_cp[d].wait_send()
    for slot in p_cp:
        p_cp[slot].wait_send()


def per_device(
    hidden_in,
    frozen_query_rows,
    new_kv,
    adapter_of,
    adapter_home,
    a_store,
    b_store,
    kv_pool,
    page_table,
    cached_len,
    new_group,
):
    groups = lax.axis_size("req")
    mps = lax.axis_size("mp")
    per_group, steps, width = hidden_in.shape
    store_count, rank, _ = a_store.shape
    pages, page = page_table.shape[1], kv_pool.shape[2]
    kv_width = kv_pool.shape[3]
    context = pages * page
    move_cap = -(-(per_group - per_group // 4) // groups)
    cap = -(-per_group // min(16, groups))
    block = -(-cap * steps // 8) * 8
    lanes = store_count * rank
    qr = width // kv_width * steps
    kv_heads = kv_width // HEAD
    moved = (groups - 1) * move_cap
    entries = per_group + moved
    bf16, f32 = jnp.bfloat16, jnp.float32
    cfg = (groups, mps, per_group, steps, cap, block, store_count, rank, pages, page, move_cap)
    dma = pltpu.SemaphoreType.DMA
    given = (
        adapter_of,
        adapter_home,
        page_table.T,
        cached_len,
        new_group,
        hidden_in,
        frozen_query_rows,
        new_kv,
        kv_pool,
        a_store.reshape(lanes, width),
        b_store.reshape(lanes, width),
    )
    att, cache = pl.pallas_call(
        functools.partial(kernel, cfg),
        out_shape=(
            jax.ShapeDtypeStruct((per_group * steps, width), bf16),
            jax.ShapeDtypeStruct((2, per_group, context, kv_width), bf16),
        ),
        in_specs=[pl.BlockSpec(memory_space=pltpu.HBM)] * len(given),
        out_specs=[pl.BlockSpec(memory_space=VMEM)] * 2,
        scratch_shapes=[SMEM(g.shape, g.dtype) for g in given[:5]]
        + [VMEM(g.shape, g.dtype) for g in given[5:]]
        + [
            dma((len(given),)),
            VMEM((groups, block, width + lanes), bf16),
            VMEM((groups, block, width + lanes), bf16),
            VMEM((groups, block, width), bf16),
            VMEM((groups, block, width), bf16),
            VMEM((groups * block, lanes), f32),
            VMEM((mps, groups * block, lanes), f32),
            VMEM((groups, block, width), bf16),
            VMEM((groups, block, width), bf16),
            VMEM((per_group, kv_heads, qr, HEAD), bf16),
            VMEM((per_group * steps, width), f32),
            VMEM((8, 128), jnp.int32),
            VMEM((groups, 8, 128), jnp.int32),
            SMEM((groups, 8, 128), jnp.int32),
            VMEM((moved, 2, context, kv_width), bf16),
            VMEM((entries, 2, context, kv_width), bf16),
            VMEM((entries, kv_heads, qr, HEAD), bf16),
            dma((groups - 1,)),
            dma((groups - 1,)),
            dma((groups - 1,)),
            dma((groups - 1,)),
            dma((mps - 1,)),
            dma((mps - 1,)),
            dma((groups - 1,)),
            dma((groups - 1,)),
            dma((groups - 1,)),
            dma((groups - 1,)),
            dma((moved,)),
            dma((moved,)),
            dma,
        ],
        compiler_params=pltpu.CompilerParams(
            collective_id=0, has_side_effects=True, vmem_limit_bytes=40 * 2**20
        ),
    )(*[pltpu.with_memory_space_constraint(g, pltpu.HBM) for g in given])
    return att.reshape(per_group, steps, width), cache


def solution(mesh):
    placed = (
        P(("rep", "req"), None, "mp"),
        P(("rep", "req"), None, "mp"),
        P(("rep", "req"), None, None, "mp"),
        P(("rep", "req")),
        P("rep"),
        P(("rep", "req"), None, "mp"),
        P(("rep", "req"), None, "mp"),
        P(None, ("rep", "req"), None, "mp"),
        P(("rep", "req"), None),
        P(("rep", "req")),
        P(("rep", "req")),
    )
    return jax.shard_map(
        per_device,
        mesh=mesh,
        in_specs=placed,
        out_specs=(P(("rep", "req"), None, "mp"), P(None, ("rep", "req"), None, "mp")),
        check_vma=False,
    )
```
